32 devices in a mesh: outer: 4 (over x, core), inner: 8 (over z, y).
Axes of the slice: x: 2, y: 2, z: 4, core: 2. Of those that a mesh axis runs over, the one named last changes fastest.
Arguments:
- vertex: float32 [131072, 128], P(('outer', 'inner')), may hold values from -1.75 to 1.75
- context: float32 [65536, 128], P(('outer', 'inner')), may hold values from -1.75 to 1.75
- tile_count: int32 [128], P(('outer', 'inner')), may hold values from 1 to 8, as said below
- tile_vert: int32 [128, 8], P(('outer', 'inner')), may hold values from 0 to 15
- tile_context: int32 [128, 8], P(('outer', 'inner')), may hold values from 0 to 7
- positives: int32 [128, 8, 256], P(('outer', 'inner')), may hold values from 0 to 255
- negatives: int32 [128, 8, 4, 256], P(('outer', 'inner')), may hold values from 0 to 255
Outputs:
- vertex_out: float32 [131072, 128], P(('outer', 'inner'))
- context_out: float32 [65536, 128], P(('outer', 'inner'))
The draws below stay inside these ranges and needn't reach their ends.
Inputs may be any that keep to these rules, and one draw needn't show every extreme that they name: `tile_count`: every entry is at least 1, and in every tour step some device has all 8 slots live.
All inputs are finite; a program needn't handle non-finite values.
Results may differ from the reference program's by a relative error of at most 0.0003.
Values sent between devices are 32-bit elements; how exact they have to be, the bound alone decides.
A program may use at most 64 MiB of HBM per device.

```python
import jax
import jax.numpy as jnp
from jax import lax

D = 128
TILE = 256
VROWS = 4096
CROWS = 2048
STEPS = 4
SLOTS = 8
NEG = 4
LISTS = 128
VTOTAL = 131072
CTOTAL = 65536
N_OUTER = 4
N_INNER = 8


def draw_tile_count(key, part):
    members = LISTS // STEPS
    counts = jax.random.randint(key, (members, STEPS), 1, SLOTS)
    chosen = jax.random.randint(jax.random.fold_in(key, 7), (STEPS,), 0, members)
    counts = counts.at[chosen, jnp.arange(STEPS)].set(SLOTS)
    return counts.reshape(LISTS).astype(jnp.int32)


def with_ends(entries, own_key, least, largest):
    dims = entries.shape
    spot = [jax.random.randint(jax.random.fold_in(own_key, axis), (), 0, dims[axis]) for axis in range(len(dims))]
    entries = entries.at[tuple(spot)].set(least)
    longest = dims.index(max(dims))
    spot[longest] = (spot[longest] + 1) % dims[longest]
    return entries.at[tuple(spot)].set(largest)


def levels(own_key, dims, split, smallest, top_value):
    def one(axis_at, parts):
        heights = jax.random.uniform(jax.random.fold_in(jax.random.fold_in(own_key, 6), axis_at), (parts,), jnp.float32, smallest / len(split), top_value / len(split))
        return jnp.repeat(jnp.exp(heights), dims[axis_at] // parts).reshape((-1,) + (1,) * (len(dims) - axis_at - 1))

    level = one(*split[0])
    for cut in split[1:]:
        level = level * one(*cut)
    return level


def centred(key, extent, spread, most, split=(), kind=jnp.bfloat16):
    gain = levels(key, extent, split, -0.22, 0.18) if split else 1.0
    entries = jax.random.normal(key, extent, jnp.float32) * spread * gain
    return jnp.minimum(jnp.maximum(entries, -most), most).astype(kind)


def setup_inputs(seed: int = 0) -> dict:
    key_of = jax.random.split(jax.random.key(seed), 8)
    return {
        "vertex": centred(key_of[0], (VTOTAL, D), 0.3, 1.75, ((0, 32),), jnp.float32),
        "context": centred(key_of[1], (CTOTAL, D), 0.3, 1.75, ((0, 32),), jnp.float32),
        "tile_count": draw_tile_count(jax.random.fold_in(key_of[7], 71), 0),
        "tile_vert": with_ends(jax.random.randint(key_of[3], (LISTS, SLOTS), 0, VROWS // TILE), jax.random.fold_in(key_of[3], 1), 0, (VROWS // TILE) - 1).astype(jnp.int32),
        "tile_context": with_ends(jax.random.randint(key_of[4], (LISTS, SLOTS), 0, CROWS // TILE), jax.random.fold_in(key_of[4], 1), 0, (CROWS // TILE) - 1).astype(jnp.int32),
        "positives": with_ends(jax.random.randint(key_of[5], (LISTS, SLOTS, TILE), 0, TILE), jax.random.fold_in(key_of[5], 1), 0, TILE - 1).astype(jnp.int32),
        "negatives": with_ends(jax.random.randint(key_of[6], (LISTS, SLOTS, NEG, TILE), 0, TILE), jax.random.fold_in(key_of[6], 1), 0, TILE - 1).astype(jnp.int32),
    }


learn_rate = 0.5


def train_rows(visiting, resident, count, tile_vert, tile_context, positives, negatives):
    slots = tile_vert.shape[0]
    width = visiting.shape[1]
    offsets = jnp.arange(TILE, dtype=jnp.int32)
    row_index = tile_vert[:, None] * TILE + offsets[None, :]
    pos_index = tile_context[:, None] * TILE + positives
    neg_index = tile_context[:, None, None] * TILE + negatives
    live = (jnp.arange(slots, dtype=jnp.int32) < count).astype(jnp.float32)
    anchor = visiting[row_index]
    pos_rows = resident[pos_index]
    neg_rows = resident[neg_index]
    pos_score = jnp.sum(anchor * pos_rows, -1)
    neg_score = jnp.sum(anchor[:, None] * neg_rows, -1)
    pos_grad = (jax.nn.sigmoid(pos_score) - 1.0) * live[:, None]
    neg_grad = jax.nn.sigmoid(neg_score) * live[:, None, None]
    vert_delta = pos_grad[..., None] * pos_rows + jnp.sum(neg_grad[..., None] * neg_rows, 1)
    vert_total = jnp.zeros_like(visiting).at[row_index.reshape(-1)].add(vert_delta.reshape(-1, width))
    context_total = jnp.zeros_like(resident).at[pos_index.reshape(-1)].add((pos_grad[..., None] * anchor).reshape(-1, width))
    context_total = context_total.at[neg_index.reshape(-1)].add((neg_grad[..., None] * anchor[:, None]).reshape(-1, width))
    return visiting - learn_rate * vert_total, resident - learn_rate * context_total


def apply_lists(operands):
    return train_rows(*operands)


def reference(vertex, context, tile_count, tile_vert, tile_context, positives, negatives):
    members = N_OUTER * N_INNER
    visiting = vertex.reshape(members, VROWS, D)
    resident = context.reshape(members, CROWS, D)
    counts = tile_count.reshape(members, STEPS)
    vert_lists = tile_vert.reshape(members, STEPS, SLOTS)
    context_lists = tile_context.reshape(members, STEPS, SLOTS)
    pos_lists = positives.reshape(members, STEPS, SLOTS, TILE)
    neg_lists = negatives.reshape(members, STEPS, SLOTS, NEG, TILE)
    for number in range(STEPS):
        visiting, resident = lax.map(apply_lists, (visiting, resident, counts[:, number], vert_lists[:, number], context_lists[:, number], pos_lists[:, number], neg_lists[:, number]))
        if number + 1 < STEPS:
            visiting = jnp.roll(visiting.reshape(N_OUTER, N_INNER, VROWS, D), 1, axis=1).reshape(members, VROWS, D)
    visiting = jnp.roll(visiting.reshape(N_OUTER, N_INNER, VROWS, D), 1, axis=0)
    return visiting.reshape(VTOTAL, D), resident.reshape(CTOTAL, D)
```

```python
import functools

import jax
import jax.numpy as jnp
from jax import lax
from jax.experimental import pallas as pl
from jax.experimental.pallas import tpu as pltpu
from jax.sharding import PartitionSpec as P

TILE = 256

learn_rate = 0.5


def halves(x):
    high = x.astype(jnp.bfloat16)
    low = (x - high.astype(jnp.float32)).astype(jnp.bfloat16)
    return high, low


def dot3(a, b, dims):
    a_high, a_low = a
    b_high, b_low = b
    dot = functools.partial(
        lax.dot_general, dimension_numbers=(dims, ((), ())), preferred_element_type=jnp.float32
    )
    return dot(a_high, b_high) + (dot(a_high, b_low) + dot(a_low, b_high))


def train(count, vert_at, context_at, positives, negatives, v_old, v_new, c_old, c_new):
    rows = lax.broadcasted_iota(jnp.int32, (TILE, TILE), 0)

    def slot(t, carry):
        at, to = vert_at(t), context_at(t)
        anchor = halves(v_old[at])
        partner = halves(c_old[to])
        scores = dot3(partner, anchor, ((1,), (1,)))
        step = -0.5 * learn_rate * jnp.tanh(0.5 * scores) - 0.5 * learn_rate
        gradient = jnp.where(positives[t] == rows, step + learn_rate, 0.0)
        for k in range(negatives.shape[1]):
            gradient += jnp.where(negatives[t, pl.ds(k, 1)] == rows, step, 0.0)
        gradient = halves(gradient)
        v_new[at] += dot3(gradient, partner, ((0,), (0,)))
        c_new[to] += dot3(gradient, anchor, ((1,), (0,)))
        return carry

    lax.fori_loop(0, count, slot, 0)


def whole_kernel(merge, *refs):
    count, vert, context_tiles, split, join = refs[:5]
    positives, negatives, c_old = refs[5:8]
    if merge:
        plus_in, minus_in, c_new, plus, minus, v_old, v_new = refs[8:]
        near = plus_in.shape[0]
        for k in range(near):
            v_old[join[k]] = plus_in[k]
            v_new[join[k]] = plus_in[k]
        for k in range(minus_in.shape[0]):
            v_old[join[near + k]] = minus_in[k]
            v_new[join[near + k]] = minus_in[k]
    else:
        v_old, c_new, plus, minus, v_new = refs[8:]
        v_new[...] = v_old[...]
    c_new[...] = c_old[...]
    train(
        count[0], lambda t: vert[t], lambda t: context_tiles[t], positives, negatives,
        v_old, v_new, c_old, c_new,
    )
    for k in range(plus.shape[0]):
        plus[k] = v_new[split[k]]
    for k in range(minus.shape[0]):
        minus[k] = v_new[split[plus.shape[0] + k]]


def near_kernel(count, vert, context_tiles, place, positives, negatives, c_old, v_old, c_new, v_new):
    v_new[...] = v_old[...]
    c_new[...] = c_old[...]
    train(
        count[0], lambda t: place[vert[t]], lambda t: context_tiles[t], positives, negatives,
        v_old, v_new, c_old, c_new,
    )


def final_kernel(join, plus, minus, out):
    near = plus.shape[0]
    for k in range(near):
        out[join[k]] = plus[k]
    for k in range(minus.shape[0]):
        out[join[near + k]] = minus[k]


SMEM = pl.BlockSpec(memory_space=pltpu.SMEM)
VMEM = pl.BlockSpec(memory_space=pltpu.VMEM)


def call(kernel, scalars, arrays, outs, scratch=()):
    return pl.pallas_call(
        kernel,
        out_shape=outs,
        in_specs=[SMEM] * len(scalars) + [VMEM] * len(arrays),
        out_specs=jax.tree.map(lambda _: VMEM, outs),
        scratch_shapes=list(scratch),
        compiler_params=pltpu.CompilerParams(vmem_limit_bytes=48 * 1024 * 1024),
        cost_estimate=pl.CostEstimate(flops=2_000_000_000, bytes_accessed=8_000_000, transcendentals=0),
    )(*scalars, *arrays)


def moved(block, by_outer, by_inner):
    outer, inner = lax.axis_size("outer"), lax.axis_size("inner")
    route = [
        (o * inner + i, (o + by_outer) % outer * inner + (i + by_inner) % inner)
        for o in range(outer)
        for i in range(inner)
    ]
    return lax.ppermute(block, ("outer", "inner"), route)


def body(vertex, context, tile_count, tile_vert, tile_context, positives, negatives):
    steps, slots = tile_vert.shape
    width = vertex.shape[1]
    tiles = vertex.shape[0] // TILE
    near = min(slots, tiles)
    far = tiles - near
    f32 = jnp.float32
    near_shape = jax.ShapeDtypeStruct((near, TILE, width), f32)
    far_shape = jax.ShapeDtypeStruct((far, TILE, width), f32)
    full = (tiles, TILE, width)

    ids = jnp.arange(tiles, dtype=jnp.int32)
    live = jnp.arange(slots, dtype=jnp.int32)[None, :] < tile_count[:, None]
    touched = jnp.any((tile_vert[:, :, None] == ids) & live[:, :, None], axis=1)
    before = (ids[None, :] < ids[:, None]).astype(jnp.int32)
    hit = touched.astype(jnp.int32)
    hits_before = jnp.sum(hit[:, None, :] * before, -1)
    place = jnp.where(touched, hits_before, jnp.sum(hit, -1, keepdims=True) + ids - hits_before)
    order = jnp.sum(jnp.where(place[:, None, :] == ids[:, None], ids, 0), -1)

    order_right = moved(order, 0, -1)
    order_left = moved(order, 0, 1)
    order_group = moved(order[steps - 1], 1, 0)

    c = context.reshape(-1, TILE, width)
    c_shape = jax.ShapeDtypeStruct(c.shape, f32)
    v = vertex.reshape(full)
    positives = positives.reshape(steps, slots, 1, TILE)
    plus = minus = None
    for s in range(steps):
        lists = [tile_count[s : s + 1], tile_vert[s], tile_context[s]]
        rows = [positives[s], negatives[s], c]
        if s % 2 == 0:
            if s == 0:
                c, plus, minus = call(
                    functools.partial(whole_kernel, False),
                    lists + [order_right[s + 1], order[0]],
                    rows + [v],
                    (c_shape, near_shape, far_shape),
                    [pltpu.VMEM(full, f32)],
                )
            else:
                c, plus, minus = call(
                    functools.partial(whole_kernel, True),
                    lists + [order_right[s + 1], order_left[s - 1]],
                    rows + [plus, minus],
                    (c_shape, near_shape, far_shape),
                    [pltpu.VMEM(full, f32), pltpu.VMEM(full, f32)],
                )
            plus = moved(plus, 0, 1)
            if s + 2 < steps:
                minus = moved(minus, 0, 2)
            else:
                minus, plus = lax.optimization_barrier((minus, plus))
                minus = moved(minus, 1, 1)
        else:
            c, plus = call(near_kernel, lists + [place[s]], rows + [plus], (c_shape, near_shape))
            if s + 1 < steps:
                plus = moved(plus, 0, 1)
            else:
                plus = moved(plus, 1, 0)
    v = call(final_kernel, [order_group], [plus, minus], jax.ShapeDtypeStruct(full, f32))
    return v.reshape(vertex.shape), c.reshape(context.shape)


def solution(mesh):
    return jax.shard_map(
        body,
        mesh=mesh,
        in_specs=(
            P(("outer", "inner"), None),
            P(("outer", "inner"), None),
            P(("outer", "inner")),
            P(("outer", "inner"), None),
            P(("outer", "inner"), None),
            P(("outer", "inner"), None, None),
            P(("outer", "inner"), None, None, None),
        ),
        out_specs=(P(("outer", "inner"), None), P(("outer", "inner"), None)),
        check_vma=False,
    )
```

```python
import functools

import jax
import jax.numpy as jnp
from jax import lax
from jax.experimental import pallas as pl
from jax.experimental.pallas import tpu as pltpu
from jax.sharding import PartitionSpec as P


TILE = 256

learn_rate = 0.5


def halves(x):
    high = x.astype(jnp.bfloat16)
    low = (x - high.astype(jnp.float32)).astype(jnp.bfloat16)
    return high, low


def dot(a, b, dims):
    return lax.dot_general(a, b, (dims, ((), ())), preferred_element_type=jnp.float32)


def ordered(tiles, slots, listed, order, place, mark):
    for k in range(tiles):
        mark[k] = 0
    for t in range(slots):
        mark[listed(t)] = 1
    found = jnp.int32(0)
    marks = [mark[k] for k in range(tiles)]
    total = functools.reduce(lambda x, y: x + y, marks)
    for k in range(tiles):
        at = jnp.where(marks[k] == 1, found, total + k - found)
        found = found + marks[k]
        order[at] = k
        if place is not None:
            place[k] = at


def train(s, count, vert_at, context_at, positives, negatives, v_old, v_new, c_old, c_new):
    rows = lax.broadcasted_iota(jnp.int32, (TILE, TILE), 0)
    slots = positives.shape[1]
    group = 2 if slots % 2 == 0 else 1
    width = v_old.shape[-1]

    def slot_group(g, carry):
        work = []
        for j in range(group):
            t = g * group + j
            live = (t < count).astype(jnp.float32)
            work.append((t, vert_at(t), context_at(t), live))
        anchors = [halves(v_old[w[1]]) for w in work]
        partners = [halves(c_old[w[2]]) for w in work]
        gradients = []
        for (t, _, _, live), (a_high, a_low), (p_high, p_low) in zip(work, anchors, partners):
            both = jnp.concatenate([a_high, a_low], 1)
            twice = jnp.concatenate([p_high, p_high], 1)
            scores = dot(twice, both, ((1,), (1,))) + dot(p_low, a_high, ((1,), (1,)))
            half = -0.5 * learn_rate * live
            step = half * jnp.tanh(0.5 * scores) + half
            gradient = jnp.where(positives[s, pl.ds(t, 1)] == rows, step + learn_rate * live, 0.0)
            for k in range(negatives.shape[2]):
                gradient += jnp.where(negatives[s, t, pl.ds(k, 1)] == rows, step, 0.0)
            gradients.append(halves(gradient))
        for (t, at, to, _), (a_high, a_low), (p_high, p_low), (g_high, g_low) in zip(
            work, anchors, partners, gradients
        ):
            wide = dot(g_high, jnp.concatenate([p_high, p_low], 1), ((0,), (0,)))
            v_new[at] += wide[:, :width] + wide[:, width:] + dot(g_low, p_high, ((0,), (0,)))
            wide = dot(g_high, jnp.concatenate([a_high, a_low], 1), ((1,), (0,)))
            c_new[to] += wide[:, :width] + wide[:, width:] + dot(g_low, a_high, ((1,), (0,)))
        return carry

    lax.fori_loop(0, (count + group - 1) // group, slot_group, 0)


def first_kernel(s, count, vert, context_tiles, positives, negatives, c_old, v_old, c_new, v_new):
    v_new[...] = v_old[...]
    c_new[...] = c_old[...]
    train(
        s, count[s], lambda t: vert[s, t], lambda t: context_tiles[s, t], positives, negatives,
        v_old, v_new, c_old, c_new,
    )


def pack_kernel(s, right, v, plus, minus, order, mark):
    tiles, near = v.shape[0], plus.shape[0]
    ordered(tiles, right.shape[1], lambda t: right[s + 1, t], order, None, mark)
    for k in range(near):
        plus[k] = v[order[k]]
    for k in range(tiles - near):
        minus[k] = v[order[near + k]]


def merge_kernel(s, *refs):
    count, vert, context_tiles, right, left = refs[:5]
    positives, negatives, c_old, plus_in, minus_in, c_new, plus, minus = refs[5:13]
    v_old, v_new, order, mark = refs[13:]
    tiles, near, slots = v_old.shape[0], plus.shape[0], vert.shape[1]
    ordered(tiles, slots, lambda t: left[s - 1, t], order, None, mark)
    for k in range(tiles):
        tile = plus_in[k] if k < near else minus_in[k - near]
        v_old[order[k]] = tile
        v_new[order[k]] = tile
    c_new[...] = c_old[...]
    train(
        s, count[s], lambda t: vert[s, t], lambda t: context_tiles[s, t], positives, negatives,
        v_old, v_new, c_old, c_new,
    )
    ordered(tiles, slots, lambda t: right[s + 1, t], order, None, mark)
    for k in range(near):
        plus[k] = v_new[order[k]]
    for k in range(tiles - near):
        minus[k] = v_new[order[near + k]]


def near_kernel(
    s, tiles, count, vert, context_tiles, positives, negatives, c_old, v_old, c_new, v_new,
    order, mark, place,
):
    ordered(tiles, vert.shape[1], lambda t: vert[s, t], order, place, mark)
    v_new[...] = v_old[...]
    c_new[...] = c_old[...]
    train(
        s, count[s], lambda t: place[vert[s, t]], lambda t: context_tiles[s, t], positives, negatives,
        v_old, v_new, c_old, c_new,
    )


def final_kernel(s, group, plus, minus, out, order, mark):
    near = plus.shape[0]
    ordered(out.shape[0], group.shape[1], lambda t: group[s, t], order, None, mark)
    for k in range(near):
        out[order[k]] = plus[k]
    for k in range(minus.shape[0]):
        out[order[near + k]] = minus[k]


SMEM = pl.BlockSpec(memory_space=pltpu.SMEM)
VMEM = pl.BlockSpec(memory_space=pltpu.VMEM)


def call(kernel, scalars, arrays, outs, scratch=()):
    return pl.pallas_call(
        kernel,
        out_shape=outs,
        in_specs=[SMEM] * len(scalars) + [VMEM] * len(arrays),
        out_specs=jax.tree.map(lambda _: VMEM, outs),
        scratch_shapes=list(scratch),
        compiler_params=pltpu.CompilerParams(vmem_limit_bytes=48 * 1024 * 1024),
        cost_estimate=pl.CostEstimate(flops=2_000_000_000, bytes_accessed=8_000_000, transcendentals=0),
    )(*scalars, *arrays)


def moved(block, by_outer, by_inner):
    outer, inner = lax.axis_size("outer"), lax.axis_size("inner")
    route = [
        (o * inner + i, (o + by_outer) % outer * inner + (i + by_inner) % inner)
        for o in range(outer)
        for i in range(inner)
    ]
    return lax.ppermute(block, ("outer", "inner"), route)


def body(vertex, context, tile_count, tile_vert, tile_context, positives, negatives):
    steps, slots = tile_vert.shape
    width = vertex.shape[1]
    tiles = vertex.shape[0] // TILE
    near = min(slots, tiles)
    far = tiles - near
    f32 = jnp.float32
    near_shape = jax.ShapeDtypeStruct((near, TILE, width), f32)
    far_shape = jax.ShapeDtypeStruct((far, TILE, width), f32)
    full = (tiles, TILE, width)

    live = jnp.arange(slots, dtype=jnp.int32)[None, :] < tile_count[:, None]
    vert = jnp.where(live, tile_vert, tile_vert[:, :1])
    right = moved(vert, 0, -1)
    left = moved(vert, 0, 1)
    group = moved(vert, 1, 0)

    c = context.reshape(-1, TILE, width)
    v = vertex.reshape(full)
    c_shape = jax.ShapeDtypeStruct(c.shape, f32)
    v_shape = jax.ShapeDtypeStruct(full, f32)
    marks = [pltpu.SMEM((tiles,), jnp.int32), pltpu.SMEM((tiles,), jnp.int32)]
    buffers = [pltpu.VMEM(full, f32), pltpu.VMEM(full, f32)]
    part = functools.partial
    lists = [tile_count, vert, tile_context]
    rows = [positives, negatives]

    c, v = call(part(first_kernel, 0), lists, rows + [c, v], (c_shape, v_shape))
    right, left, group, v = lax.optimization_barrier((right, left, group, v))
    plus, minus = call(part(pack_kernel, 0), [right], [v], (near_shape, far_shape), marks)
    for s in range(steps):
        if s % 2 == 0:
            if s > 0:
                c, plus, minus = call(
                    part(merge_kernel, s), lists + [right, left], rows + [c, plus, minus],
                    (c_shape, near_shape, far_shape), buffers + marks,
                )
            plus = moved(plus, 0, 1)
            minus = moved(minus, 0, 2) if s + 2 < steps else moved(minus, 1, 1)
        else:
            c, plus = call(
                part(near_kernel, s, tiles), lists, rows + [c, plus], (c_shape, near_shape),
                marks + marks[:1],
            )
            if s + 1 < steps:
                plus = moved(plus, 0, 1)
            else:
                plus = moved(plus, 1, 0)
    v = call(part(final_kernel, steps - 1), [group], [plus, minus], v_shape, marks)
    return v.reshape(vertex.shape), c.reshape(context.shape)


def solution(mesh):
    return jax.shard_map(
        body,
        mesh=mesh,
        in_specs=(
            P(("outer", "inner"), None),
            P(("outer", "inner"), None),
            P(("outer", "inner")),
            P(("outer", "inner"), None),
            P(("outer", "inner"), None),
            P(("outer", "inner"), None, None),
            P(("outer", "inner"), None, None, None),
        ),
        out_specs=(P(("outer", "inner"), None), P(("outer", "inner"), None)),
        check_vma=False,
    )
```

```python
import functools

import jax
import jax.numpy as jnp
from jax import lax
from jax.experimental import pallas as pl
from jax.experimental.pallas import tpu as pltpu
from jax.sharding import PartitionSpec as P


TILE = 256

learn_rate = 0.5


def halves(x):
    high = x.astype(jnp.bfloat16)
    low = (x - high.astype(jnp.float32)).astype(jnp.bfloat16)
    return high, low


def dot(a, b, dims):
    return lax.dot_general(a, b, (dims, ((), ())), preferred_element_type=jnp.float32)


def ordered(tiles, slots, listed, order, place, mark):
    for k in range(tiles):
        mark[k] = 0
    for t in range(slots):
        tile = listed(t)
        mark[jnp.where(tile < 0, listed(0), tile)] = 1
    found = jnp.int32(0)
    marks = [mark[k] for k in range(tiles)]
    total = functools.reduce(lambda x, y: x + y, marks)
    for k in range(tiles):
        at = jnp.where(marks[k] == 1, found, total + k - found)
        found = found + marks[k]
        order[at] = k
        if place is not None:
            place[k] = at


def train(s, count, vert_at, context_at, positives, negatives, v_old, v_new, c_old, c_new):
    rows = lax.broadcasted_iota(jnp.int32, (TILE, TILE), 0)
    slots = positives.shape[1]
    group = 2 if slots % 2 == 0 else 1
    width = v_old.shape[-1]

    def slot_group(g, carry):
        work = []
        for j in range(group):
            t = g * group + j
            live = (t < count).astype(jnp.float32)
            work.append((t, vert_at(jnp.where(t < count, t, 0)), context_at(t), live))
        anchors = [halves(v_old[w[1]]) for w in work]
        partners = [halves(c_old[w[2]]) for w in work]
        gradients = []
        for (t, _, _, live), (a_high, a_low), (p_high, p_low) in zip(work, anchors, partners):
            both = jnp.concatenate([a_high, a_low], 1)
            twice = jnp.concatenate([p_high, p_high], 1)
            scores = dot(twice, both, ((1,), (1,))) + dot(p_low, a_high, ((1,), (1,)))
            half = -0.5 * learn_rate * live
            step = half * jnp.tanh(0.5 * scores) + half
            gradient = jnp.where(positives[s, pl.ds(t, 1)] == rows, step + learn_rate * live, 0.0)
            for k in range(negatives.shape[2]):
                gradient += jnp.where(negatives[s, t, pl.ds(k, 1)] == rows, step, 0.0)
            gradients.append(halves(gradient))
        for (t, at, to, _), (a_high, a_low), (p_high, p_low), (g_high, g_low) in zip(
            work, anchors, partners, gradients
        ):
            wide = dot(g_high, jnp.concatenate([p_high, p_low], 1), ((0,), (0,)))
            v_new[at] += wide[:, :width] + wide[:, width:] + dot(g_low, p_high, ((0,), (0,)))
            wide = dot(g_high, jnp.concatenate([a_high, a_low], 1), ((1,), (0,)))
            c_new[to] += wide[:, :width] + wide[:, width:] + dot(g_low, a_high, ((1,), (0,)))
        return carry

    lax.fori_loop(0, (count + group - 1) // group, slot_group, 0)


def split(v, order, plus, minus):
    near = plus.shape[0]
    for k in range(near):
        plus[k] = v[order[k]]
    for k in range(minus.shape[0]):
        minus[k] = v[order[near + k]]


def first_kernel(
    s, count, vert, context_tiles, right, positives_hbm, negatives_hbm, c_hbm, v_hbm,
    c_new, plus, minus, positives, negatives, c_old, v_old, v_new, order, mark, sems,
):
    copies = [
        pltpu.make_async_copy(source, target, sems.at[k])
        for k, (source, target) in enumerate(
            (
                (v_hbm, v_old),
                (c_hbm, c_old),
                (positives_hbm.at[pl.ds(s, 1)], positives),
                (negatives_hbm.at[pl.ds(s, 1)], negatives),
            )
        )
    ]
    for copy in copies:
        copy.start()
    ordered(v_old.shape[0], vert.shape[1], lambda t: right[s + 1, t], order, None, mark)
    for copy in copies:
        copy.wait()
    v_new[...] = v_old[...]
    c_new[...] = c_old[...]
    train(
        0, count[s], lambda t: vert[s, t], lambda t: context_tiles[s, t], positives, negatives,
        v_old, v_new, c_old, c_new,
    )
    split(v_new, order, plus, minus)


def merge_kernel(s, *refs):
    count, vert, context_tiles, right, left, odd = refs[:6]
    positives, negatives, c_old, direct, swapped, relayed, minus_in = refs[6:13]
    c_new, plus, minus, v_old, v_new, order, mark = refs[13:]
    tiles, near, slots = v_old.shape[0], plus.shape[0], vert.shape[1]
    first = direct.shape[0]
    ordered(tiles, slots, lambda t: left[s - 1, t], order, None, mark)

    def put(k, tile):
        v_old[order[k]] = tile
        v_new[order[k]] = tile

    for k in range(first):
        put(k, direct[k])
    for k in range(near, tiles):
        put(k, minus_in[k - near])

    @pl.when(odd[0] == 1)
    def _():
        for k in range(first, near):
            put(k, swapped[k - first])

    @pl.when(odd[0] == 0)
    def _():
        for k in range(first, near):
            put(k, relayed[k - first])

    c_new[...] = c_old[...]
    train(
        s, count[s], lambda t: vert[s, t], lambda t: context_tiles[s, t], positives, negatives,
        v_old, v_new, c_old, c_new,
    )
    ordered(tiles, slots, lambda t: right[s + 1, t], order, None, mark)
    split(v_new, order, plus, minus)


def near_kernel(s, tiles, *refs):
    count, vert, context_tiles, positives, negatives, c_old, v_old, c_new = refs[:8]
    outs, (v_new, order, mark, place) = refs[8:-4], refs[-4:]
    ordered(tiles, vert.shape[1], lambda t: vert[s, t], order, place, mark)
    v_new[...] = v_old[...]
    c_new[...] = c_old[...]
    train(
        s, count[s], lambda t: place[vert[s, t]], lambda t: context_tiles[s, t], positives, negatives,
        v_old, v_new, c_old, c_new,
    )
    start = 0
    for out in outs:
        out[...] = v_new[pl.ds(start, out.shape[0])]
        start += out.shape[0]


def final_kernel(s, group, plus, minus, out, order, mark):
    near = plus.shape[0]
    ordered(out.shape[0], group.shape[1], lambda t: group[s, t], order, None, mark)
    for k in range(near):
        out[order[k]] = plus[k]
    for k in range(minus.shape[0]):
        out[order[near + k]] = minus[k]


SMEM = pl.BlockSpec(memory_space=pltpu.SMEM)
VMEM = pl.BlockSpec(memory_space=pltpu.VMEM)


HBM = pl.BlockSpec(memory_space=pltpu.HBM)


def call(kernel, scalars, arrays, outs, scratch=(), space=VMEM, limit=20):
    return pl.pallas_call(
        kernel,
        out_shape=outs,
        in_specs=[SMEM] * len(scalars) + [space] * len(arrays),
        out_specs=jax.tree.map(lambda _: VMEM, outs),
        scratch_shapes=list(scratch),
        compiler_params=pltpu.CompilerParams(vmem_limit_bytes=limit * 1024 * 1024),
        cost_estimate=pl.CostEstimate(flops=2_000_000_000, bytes_accessed=8_000_000, transcendentals=0),
    )(*scalars, *arrays)


def moved(block, by_outer, by_inner, taken=lambda i: True):
    outer, inner = lax.axis_size("outer"), lax.axis_size("inner")
    target = by_inner if callable(by_inner) else lambda i: (i + by_inner) % inner
    route = [
        (o * inner + i, (o + by_outer) % outer * inner + target(i))
        for o in range(outer)
        for i in range(inner)
        if taken(i)
    ]
    return lax.ppermute(block, ("outer", "inner"), route)


def body(vertex, context, tile_count, tile_vert, tile_context, positives, negatives):
    steps, slots = tile_vert.shape
    width = vertex.shape[1]
    tiles = vertex.shape[0] // TILE
    near = min(slots, tiles)
    far = tiles - near
    f32 = jnp.float32
    near_shape = jax.ShapeDtypeStruct((near, TILE, width), f32)
    far_shape = jax.ShapeDtypeStruct((far, TILE, width), f32)
    full = (tiles, TILE, width)

    live = jnp.arange(slots, dtype=jnp.int32)[None, :] < tile_count[:, None]
    vert = jnp.where(live, tile_vert, -1)
    right = moved(vert, 0, -1)
    odd = lax.rem(lax.axis_index("inner"), 2).reshape(1)

    c = context.reshape(-1, TILE, width)
    v = vertex.reshape(full)
    c_shape = jax.ShapeDtypeStruct(c.shape, f32)
    v_shape = jax.ShapeDtypeStruct(full, f32)
    marks = [pltpu.SMEM((tiles,), jnp.int32), pltpu.SMEM((tiles,), jnp.int32)]
    buffers = [pltpu.VMEM(full, f32), pltpu.VMEM(full, f32)]
    part = functools.partial
    lists = [tile_count, vert, tile_context]
    rows = [positives, negatives]

    c, plus, minus = call(
        part(first_kernel, 0), lists + [right], rows + [c, v], (c_shape, near_shape, far_shape),
        [
            pltpu.VMEM((1,) + positives.shape[1:], jnp.int32),
            pltpu.VMEM((1,) + negatives.shape[1:], jnp.int32),
            pltpu.VMEM(c.shape, f32),
            pltpu.VMEM(full, f32),
            pltpu.VMEM(full, f32),
        ]
        + marks
        + [pltpu.SemaphoreType.DMA((4,))],
        HBM,
        62,
    )
    late, plus = lax.optimization_barrier((vert, plus))
    near_buffer = [pltpu.VMEM(near_shape.shape, f32)]
    half = near // 2
    halves_shape = tuple(
        jax.ShapeDtypeStruct((size, TILE, width), f32) for size in (half, near - half)
    )
    for s in range(steps):
        if s % 2 == 0:
            if s > 0:
                c, plus, minus = call(
                    part(merge_kernel, s), lists + [right, left, odd],
                    rows + [c, direct, swapped, relayed, minus],
                    (c_shape, near_shape, far_shape), buffers + marks,
                )
            plus = moved(plus, 0, 1)
            minus = moved(minus, 0, 2) if s + 2 < steps else moved(minus, 1, 1)
            if s == 0:
                left = moved(late, 0, 1)
                group = moved(late, 1, 0)
        else:
            outs = halves_shape if s + 1 < steps else (near_shape,)
            c, *parts = call(
                part(near_kernel, s, tiles), lists, rows + [c, plus], (c_shape,) + outs,
                near_buffer + marks + marks[:1],
            )
            if s + 1 < steps:
                direct, swapped = parts
                swapped = moved(swapped, 0, lambda i: i ^ 1)
                direct = moved(direct, 0, 1)
                relayed = moved(swapped, 0, 2, lambda i: i % 2 == 0)
            else:
                plus = moved(parts[0], 1, 0)
    v = call(part(final_kernel, steps - 1), [group], [plus, minus], v_shape, marks)
    return v.reshape(vertex.shape), c.reshape(context.shape)


def solution(mesh):
    return jax.shard_map(
        body,
        mesh=mesh,
        in_specs=(
            P(("outer", "inner"), None),
            P(("outer", "inner"), None),
            P(("outer", "inner")),
            P(("outer", "inner"), None),
            P(("outer", "inner"), None),
            P(("outer", "inner"), None, None),
            P(("outer", "inner"), None, None, None),
        ),
        out_specs=(P(("outer", "inner"), None), P(("outer", "inner"), None)),
        check_vma=False,
    )
```

```python
import functools

import jax
import jax.numpy as jnp
from jax import lax
from jax.experimental import pallas as pl
from jax.experimental.pallas import tpu as pltpu
from jax.sharding import PartitionSpec as P


TILE = 256

learn_rate = 0.5


def halves(x):
    high = x.astype(jnp.bfloat16)
    low = (x - high.astype(jnp.float32)).astype(jnp.bfloat16)
    return high, low


def dot(a, b, dims):
    return lax.dot_general(a, b, (dims, ((), ())), preferred_element_type=jnp.float32)


def ordered(tiles, slots, listed, order, place, mark):
    for k in range(tiles):
        mark[k] = 0
    for t in range(slots):
        tile = listed(t)
        mark[jnp.where(tile < 0, listed(0), tile)] = 1
    found = jnp.int32(0)
    marks = [mark[k] for k in range(tiles)]
    total = functools.reduce(lambda x, y: x + y, marks)
    for k in range(tiles):
        at = jnp.where(marks[k] == 1, found, total + k - found)
        found = found + marks[k]
        order[at] = k
        if place is not None:
            place[k] = at


def train(s, count, vert_at, context_at, positives, negatives, v_old, v_new, c_old, c_new):
    rows = lax.broadcasted_iota(jnp.int32, (TILE, TILE), 0)
    slots = positives.shape[1]
    group = 2 if slots % 2 == 0 else 1
    width = v_old.shape[-1]

    def slot_group(g, carry):
        work = []
        for j in range(group):
            t = g * group + j
            live = (t < count).astype(jnp.float32)
            work.append((t, vert_at(jnp.where(t < count, t, 0)), context_at(t), live))
        anchors = [halves(v_old[w[1]]) for w in work]
        partners = [halves(c_old[w[2]]) for w in work]
        gradients = []
        for (t, _, _, live), (a_high, a_low), (p_high, p_low) in zip(work, anchors, partners):
            both = jnp.concatenate([a_high, a_low], 1)
            twice = jnp.concatenate([p_high, p_high], 1)
            scores = dot(twice, both, ((1,), (1,))) + dot(p_low, a_high, ((1,), (1,)))
            half = -0.5 * learn_rate * live
            step = half * jnp.tanh(0.5 * scores) + half
            gradient = jnp.where(positives[s, pl.ds(t, 1)] == rows, step + learn_rate * live, 0.0)
            for k in range(negatives.shape[2]):
                gradient += jnp.where(negatives[s, t, pl.ds(k, 1)] == rows, step, 0.0)
            gradients.append(halves(gradient))
        for (t, at, to, _), (a_high, a_low), (p_high, p_low), (g_high, g_low) in zip(
            work, anchors, partners, gradients
        ):
            wide = dot(g_high, jnp.concatenate([p_high, p_low], 1), ((0,), (0,)))
            v_new[at] += wide[:, :width] + wide[:, width:] + dot(g_low, p_high, ((0,), (0,)))
            wide = dot(g_high, jnp.concatenate([a_high, a_low], 1), ((1,), (0,)))
            c_new[to] += wide[:, :width] + wide[:, width:] + dot(g_low, a_high, ((1,), (0,)))
        return carry

    lax.fori_loop(0, (count + group - 1) // group, slot_group, 0)


def split(v, order, plus, minus):
    near = plus.shape[0]
    for k in range(near):
        plus[k] = v[order[k]]
    for k in range(minus.shape[0]):
        minus[k] = v[order[near + k]]


def first_kernel(
    s, count, vert, context_tiles, right, positives_hbm, negatives_hbm, c_hbm, v_hbm,
    c_new, plus, minus, positives, negatives, c_old, v_old, v_new, order, mark, sems,
):
    copies = [
        pltpu.make_async_copy(source, target, sems.at[k])
        for k, (source, target) in enumerate(
            (
                (v_hbm, v_old),
                (c_hbm, c_old),
                (positives_hbm.at[pl.ds(s, 1)], positives),
                (negatives_hbm.at[pl.ds(s, 1)], negatives),
            )
        )
    ]
    for copy in copies:
        copy.start()
    ordered(v_old.shape[0], vert.shape[1], lambda t: right[s + 1, t], order, None, mark)
    for copy in copies:
        copy.wait()
    v_new[...] = v_old[...]
    c_new[...] = c_old[...]
    train(
        0, count[s], lambda t: vert[s, t], lambda t: context_tiles[s, t], positives, negatives,
        v_old, v_new, c_old, c_new,
    )
    split(v_new, order, plus, minus)


def merge_kernel(s, *refs):
    count, vert, context_tiles, right, left, odd = refs[:6]
    positives, negatives, c_old, direct, swapped, relayed, minus_in = refs[6:13]
    c_new, plus, minus, v_old, v_new, order, mark = refs[13:]
    tiles, near, slots = v_old.shape[0], plus.shape[0], vert.shape[1]
    first = direct.shape[0]
    ordered(tiles, slots, lambda t: left[s - 1, t], order, None, mark)

    def put(k, tile):
        v_old[order[k]] = tile
        v_new[order[k]] = tile

    for k in range(first):
        put(k, direct[k])
    for k in range(near, tiles):
        put(k, minus_in[k - near])

    @pl.when(odd[0] == 1)
    def _():
        for k in range(first, near):
            put(k, swapped[k - first])

    @pl.when(odd[0] == 0)
    def _():
        for k in range(first, near):
            put(k, relayed[k - first])

    c_new[...] = c_old[...]
    train(
        s, count[s], lambda t: vert[s, t], lambda t: context_tiles[s, t], positives, negatives,
        v_old, v_new, c_old, c_new,
    )
    ordered(tiles, slots, lambda t: right[s + 1, t], order, None, mark)
    split(v_new, order, plus, minus)


def near_kernel(s, tiles, *refs):
    count, vert, context_tiles, positives, negatives, c_old, v_old, c_new = refs[:8]
    outs, (v_new, order, mark, place) = refs[8:-4], refs[-4:]
    ordered(tiles, vert.shape[1], lambda t: vert[s, t], order, place, mark)
    v_new[...] = v_old[...]
    c_new[...] = c_old[...]
    train(
        s, count[s], lambda t: place[vert[s, t]], lambda t: context_tiles[s, t], positives, negatives,
        v_old, v_new, c_old, c_new,
    )
    start = 0
    for out in outs:
        out[...] = v_new[pl.ds(start, out.shape[0])]
        start += out.shape[0]


def final_kernel(s, group, plus, minus, out, order, mark, sems):
    near, tiles = plus.shape[0], out.shape[0]
    ordered(tiles, group.shape[1], lambda t: group[s, t], order, None, mark)
    copies = [
        pltpu.make_async_copy(
            plus.at[k] if k < near else minus.at[k - near], out.at[order[k]], sems.at[k]
        )
        for k in range(tiles)
    ]
    for copy in copies:
        copy.start()
    for copy in copies:
        copy.wait()


SMEM = pl.BlockSpec(memory_space=pltpu.SMEM)
VMEM = pl.BlockSpec(memory_space=pltpu.VMEM)


HBM = pl.BlockSpec(memory_space=pltpu.HBM)


def call(kernel, scalars, arrays, outs, scratch=(), space=VMEM, limit=20, out_space=VMEM):
    return pl.pallas_call(
        kernel,
        out_shape=outs,
        in_specs=[SMEM] * len(scalars) + [space] * len(arrays),
        out_specs=jax.tree.map(lambda _: out_space, outs),
        scratch_shapes=list(scratch),
        compiler_params=pltpu.CompilerParams(vmem_limit_bytes=limit * 1024 * 1024),
        cost_estimate=pl.CostEstimate(flops=2_000_000_000, bytes_accessed=8_000_000, transcendentals=0),
    )(*scalars, *arrays)


def moved(block, by_outer, by_inner, taken=lambda i: True):
    outer, inner = lax.axis_size("outer"), lax.axis_size("inner")
    target = by_inner if callable(by_inner) else lambda i: (i + by_inner) % inner
    route = [
        (o * inner + i, (o + by_outer) % outer * inner + target(i))
        for o in range(outer)
        for i in range(inner)
        if taken(i)
    ]
    return lax.ppermute(block, ("outer", "inner"), route)


def body(vertex, context, tile_count, tile_vert, tile_context, positives, negatives):
    steps, slots = tile_vert.shape
    width = vertex.shape[1]
    tiles = vertex.shape[0] // TILE
    near = min(slots, tiles)
    far = tiles - near
    f32 = jnp.float32
    near_shape = jax.ShapeDtypeStruct((near, TILE, width), f32)
    far_shape = jax.ShapeDtypeStruct((far, TILE, width), f32)
    full = (tiles, TILE, width)

    live = jnp.arange(slots, dtype=jnp.int32)[None, :] < tile_count[:, None]
    vert = jnp.where(live, tile_vert, -1)
    right = moved(vert, 0, -1)
    odd = lax.rem(lax.axis_index("inner"), 2).reshape(1)

    c = context.reshape(-1, TILE, width)
    v = vertex.reshape(full)
    c_shape = jax.ShapeDtypeStruct(c.shape, f32)
    v_shape = jax.ShapeDtypeStruct(full, f32)
    marks = [pltpu.SMEM((tiles,), jnp.int32), pltpu.SMEM((tiles,), jnp.int32)]
    buffers = [pltpu.VMEM(full, f32), pltpu.VMEM(full, f32)]
    part = functools.partial
    lists = [tile_count, vert, tile_context]
    rows = [positives, negatives]

    c, plus, minus = call(
        part(first_kernel, 0), lists + [right], rows + [c, v], (c_shape, near_shape, far_shape),
        [
            pltpu.VMEM((1,) + positives.shape[1:], jnp.int32),
            pltpu.VMEM((1,) + negatives.shape[1:], jnp.int32),
            pltpu.VMEM(c.shape, f32),
            pltpu.VMEM(full, f32),
            pltpu.VMEM(full, f32),
        ]
        + marks
        + [pltpu.SemaphoreType.DMA((4,))],
        HBM,
        62,
    )
    late, plus = lax.optimization_barrier((vert, plus))
    near_buffer = [pltpu.VMEM(near_shape.shape, f32)]
    half = near // 2
    halves_shape = tuple(
        jax.ShapeDtypeStruct((size, TILE, width), f32) for size in (half, near - half)
    )
    for s in range(steps):
        if s % 2 == 0:
            if s > 0:
                c, plus, minus = call(
                    part(merge_kernel, s), lists + [right, left, odd],
                    rows + [c, direct, swapped, relayed, minus],
                    (c_shape, near_shape, far_shape), buffers + marks,
                )
            plus = moved(plus, 0, 1)
            minus = moved(minus, 0, 2) if s + 2 < steps else moved(minus, 1, 1)
            if s == 0:
                left = moved(late, 0, 1)
                group = moved(late, 1, 0)
        else:
            outs = halves_shape if s + 1 < steps else (near_shape,)
            c, *parts = call(
                part(near_kernel, s, tiles), lists, rows + [c, plus], (c_shape,) + outs,
                near_buffer + marks + marks[:1],
            )
            if s + 1 < steps:
                direct, swapped = parts
                swapped = moved(swapped, 0, lambda i: i ^ 1)
                direct = moved(direct, 0, 1)
                relayed = moved(swapped, 0, 2, lambda i: i % 2 == 0)
            else:
                plus = moved(parts[0], 1, 0)
    v = call(
        part(final_kernel, steps - 1), [group], [plus, minus], v_shape,
        marks + [pltpu.SemaphoreType.DMA((tiles,))], out_space=HBM,
    )
    return v.reshape(vertex.shape), c.reshape(context.shape)


def solution(mesh):
    return jax.shard_map(
        body,
        mesh=mesh,
        in_specs=(
            P(("outer", "inner"), None),
            P(("outer", "inner"), None),
            P(("outer", "inner")),
            P(("outer", "inner"), None),
            P(("outer", "inner"), None),
            P(("outer", "inner"), None, None),
            P(("outer", "inner"), None, None, None),
        ),
        out_specs=(P(("outer", "inner"), None), P(("outer", "inner"), None)),
        check_vma=False,
    )
```

```python
import functools

import jax
import jax.numpy as jnp
from jax import lax
from jax.experimental import pallas as pl
from jax.experimental.pallas import tpu as pltpu
from jax.sharding import PartitionSpec as P


TILE = 256

learn_rate = 0.5


def halves(x):
    high = x.astype(jnp.bfloat16)
    low = (x - high.astype(jnp.float32)).astype(jnp.bfloat16)
    return high, low


def dot(a, b, dims):
    return lax.dot_general(a, b, (dims, ((), ())), preferred_element_type=jnp.float32)


def ordered(tiles, slots, listed, order, place, mark):
    for k in range(tiles):
        mark[k] = 0
    for t in range(slots):
        tile = listed(t)
        mark[jnp.where(tile < 0, listed(0), tile)] = 1
    found = jnp.int32(0)
    marks = [mark[k] for k in range(tiles)]
    total = functools.reduce(lambda x, y: x + y, marks)
    for k in range(tiles):
        at = jnp.where(marks[k] == 1, found, total + k - found)
        found = found + marks[k]
        order[at] = k
        if place is not None:
            place[k] = at


def train(s, count, vert_at, context_at, positives, negatives, v_old, v_new, c_old, c_new):
    rows = lax.broadcasted_iota(jnp.int32, (TILE, TILE), 0)
    slots = positives.shape[1]
    group = 2 if slots % 2 == 0 else 1
    width = v_old.shape[-1]

    def slot_group(g, carry):
        work = []
        for j in range(group):
            t = g * group + j
            live = (t < count).astype(jnp.float32)
            work.append((t, vert_at(jnp.where(t < count, t, 0)), context_at(t), live))
        anchors = [halves(v_old[w[1]]) for w in work]
        partners = [halves(c_old[w[2]]) for w in work]
        gradients = []
        for (t, _, _, live), (a_high, a_low), (p_high, p_low) in zip(work, anchors, partners):
            both = jnp.concatenate([a_high, a_low], 1)
            twice = jnp.concatenate([p_high, p_high], 1)
            scores = dot(twice, both, ((1,), (1,))) + dot(p_low, a_high, ((1,), (1,)))
            half = -0.5 * learn_rate * live
            step = half * jnp.tanh(0.5 * scores) + half
            gradient = jnp.where(positives[s, pl.ds(t, 1)] == rows, step + learn_rate * live, 0.0)
            for k in range(negatives.shape[2]):
                gradient += jnp.where(negatives[s, t, pl.ds(k, 1)] == rows, step, 0.0)
            gradients.append(halves(gradient))
        for (t, at, to, _), (a_high, a_low), (p_high, p_low), (g_high, g_low) in zip(
            work, anchors, partners, gradients
        ):
            wide = dot(g_high, jnp.concatenate([p_high, p_low], 1), ((0,), (0,)))
            v_new[at] += wide[:, :width] + wide[:, width:] + dot(g_low, p_high, ((0,), (0,)))
            wide = dot(g_high, jnp.concatenate([a_high, a_low], 1), ((1,), (0,)))
            c_new[to] += wide[:, :width] + wide[:, width:] + dot(g_low, a_high, ((1,), (0,)))
        return carry

    lax.fori_loop(0, (count + group - 1) // group, slot_group, 0)


def split(v, order, outs):
    start = 0
    for out in outs:
        for k in range(out.shape[0]):
            out[k] = v[order[start + k]]
        start += out.shape[0]


def first_kernel(
    s, count, vert, context_tiles, right, positives_hbm, negatives_hbm, c_hbm, v_hbm,
    c_new, plus, minus, positives, negatives, c_old, v_old, v_new, order, mark, sems,
):
    copies = [
        pltpu.make_async_copy(source, target, sems.at[k])
        for k, (source, target) in enumerate(
            (
                (v_hbm, v_old),
                (c_hbm, c_old),
                (positives_hbm.at[pl.ds(s, 1)], positives),
                (negatives_hbm.at[pl.ds(s, 1)], negatives),
            )
        )
    ]
    for copy in copies:
        copy.start()
    ordered(v_old.shape[0], vert.shape[1], lambda t: right[s + 1, t], order, None, mark)
    for copy in copies:
        copy.wait()
    v_new[...] = v_old[...]
    c_new[...] = c_old[...]
    train(
        0, count[s], lambda t: vert[s, t], lambda t: context_tiles[s, t], positives, negatives,
        v_old, v_new, c_old, c_new,
    )
    split(v_new, order, (plus, minus))


def merge_kernel(s, *refs):
    count, vert, context_tiles, right, left, odd = refs[:6]
    positives, negatives, c_old, direct, swapped, relayed, minus_in = refs[6:13]
    c_new, plus, *minus, v_old, v_new, order, mark = refs[13:]
    tiles, near, slots = v_old.shape[0], plus.shape[0], vert.shape[1]
    first = direct.shape[0]
    ordered(tiles, slots, lambda t: left[s - 1, t], order, None, mark)

    def put(k, tile):
        v_old[order[k]] = tile
        v_new[order[k]] = tile

    for k in range(first):
        put(k, direct[k])
    for k in range(near, tiles):
        put(k, minus_in[k - near])

    @pl.when(odd[0] == 1)
    def _():
        for k in range(first, near):
            put(k, swapped[k - first])

    @pl.when(odd[0] == 0)
    def _():
        for k in range(first, near):
            put(k, relayed[k - first])

    c_new[...] = c_old[...]
    train(
        s, count[s], lambda t: vert[s, t], lambda t: context_tiles[s, t], positives, negatives,
        v_old, v_new, c_old, c_new,
    )
    ordered(tiles, slots, lambda t: right[s + 1, t], order, None, mark)
    split(v_new, order, (plus, *minus))


def near_kernel(s, tiles, *refs):
    count, vert, context_tiles, positives, negatives, c_old, v_old, c_new = refs[:8]
    outs, (v_new, order, mark, place) = refs[8:-4], refs[-4:]
    ordered(tiles, vert.shape[1], lambda t: vert[s, t], order, place, mark)
    v_new[...] = v_old[...]
    c_new[...] = c_old[...]
    train(
        s, count[s], lambda t: place[vert[s, t]], lambda t: context_tiles[s, t], positives, negatives,
        v_old, v_new, c_old, c_new,
    )
    start = 0
    for out in outs:
        out[...] = v_new[pl.ds(start, out.shape[0])]
        start += out.shape[0]


def final_kernel(s, group, plus, early, minus, out, order, mark, sems):
    tiles = out.shape[0]
    ordered(tiles, group.shape[1], lambda t: group[s, t], order, None, mark)
    sources = [part.at[k] for part in (plus, early, minus) for k in range(part.shape[0])]
    copies = [
        pltpu.make_async_copy(sources[k], out.at[order[k]], sems.at[k]) for k in range(tiles)
    ]
    for copy in copies:
        copy.start()
    for copy in copies:
        copy.wait()


SMEM = pl.BlockSpec(memory_space=pltpu.SMEM)
VMEM = pl.BlockSpec(memory_space=pltpu.VMEM)


HBM = pl.BlockSpec(memory_space=pltpu.HBM)


def call(kernel, scalars, arrays, outs, scratch=(), space=VMEM, limit=20, out_space=VMEM):
    return pl.pallas_call(
        kernel,
        out_shape=outs,
        in_specs=[SMEM] * len(scalars) + [space] * len(arrays),
        out_specs=jax.tree.map(lambda _: out_space, outs),
        scratch_shapes=list(scratch),
        compiler_params=pltpu.CompilerParams(vmem_limit_bytes=limit * 1024 * 1024),
        cost_estimate=pl.CostEstimate(flops=2_000_000_000, bytes_accessed=8_000_000, transcendentals=0),
    )(*scalars, *arrays)


def moved(block, by_outer, by_inner, taken=lambda i: True):
    outer, inner = lax.axis_size("outer"), lax.axis_size("inner")
    target = by_inner if callable(by_inner) else lambda i: (i + by_inner) % inner
    route = [
        (o * inner + i, (o + by_outer) % outer * inner + target(i))
        for o in range(outer)
        for i in range(inner)
        if taken(i)
    ]
    return lax.ppermute(block, ("outer", "inner"), route)


def body(vertex, context, tile_count, tile_vert, tile_context, positives, negatives):
    steps, slots = tile_vert.shape
    width = vertex.shape[1]
    tiles = vertex.shape[0] // TILE
    near = min(slots, tiles)
    far = tiles - near
    f32 = jnp.float32
    near_shape = jax.ShapeDtypeStruct((near, TILE, width), f32)
    far_shape = jax.ShapeDtypeStruct((far, TILE, width), f32)
    full = (tiles, TILE, width)

    live = jnp.arange(slots, dtype=jnp.int32)[None, :] < tile_count[:, None]
    vert = jnp.where(live, tile_vert, -1)
    right = moved(vert, 0, -1)
    odd = lax.rem(lax.axis_index("inner"), 2).reshape(1)

    c = context.reshape(-1, TILE, width)
    v = vertex.reshape(full)
    c_shape = jax.ShapeDtypeStruct(c.shape, f32)
    v_shape = jax.ShapeDtypeStruct(full, f32)
    marks = [pltpu.SMEM((tiles,), jnp.int32), pltpu.SMEM((tiles,), jnp.int32)]
    buffers = [pltpu.VMEM(full, f32), pltpu.VMEM(full, f32)]
    part = functools.partial
    lists = [tile_count, vert, tile_context]
    rows = [positives, negatives]

    c, plus, minus = call(
        part(first_kernel, 0), lists + [right], rows + [c, v], (c_shape, near_shape, far_shape),
        [
            pltpu.VMEM((1,) + positives.shape[1:], jnp.int32),
            pltpu.VMEM((1,) + negatives.shape[1:], jnp.int32),
            pltpu.VMEM(c.shape, f32),
            pltpu.VMEM(full, f32),
            pltpu.VMEM(full, f32),
        ]
        + marks
        + [pltpu.SemaphoreType.DMA((4,))],
        HBM,
        62,
    )
    late, plus = lax.optimization_barrier((vert, plus))
    near_buffer = [pltpu.VMEM(near_shape.shape, f32)]
    half = near // 2
    halves_shape = tuple(
        jax.ShapeDtypeStruct((size, TILE, width), f32) for size in (half, near - half)
    )
    for s in range(steps):
        if s % 2 == 0:
            if s > 0:
                more = s + 2 < steps
                far_shapes = (far_shape,) if more else tuple(
                    jax.ShapeDtypeStruct((size, TILE, width), f32)
                    for size in (far // 2, far - far // 2)
                )
                c, plus, *minuses = call(
                    part(merge_kernel, s), lists + [right, left, odd],
                    rows + [c, direct, swapped, relayed, minus],
                    (c_shape, near_shape) + far_shapes, buffers + marks,
                )
            plus = moved(plus, 0, 1)
            if s > 0:
                minus = minuses[-1]
            minus = moved(minus, 0, 2) if s + 2 < steps else moved(minus, 1, 1)
            if s > 0 and s + 2 >= steps:
                early = moved(minuses[0], 1, 1)
            if s == 0:
                left = moved(late, 0, 1)
                group = moved(late, 1, 0)
        else:
            outs = halves_shape if s + 1 < steps else (near_shape,)
            c, *parts = call(
                part(near_kernel, s, tiles), lists, rows + [c, plus], (c_shape,) + outs,
                near_buffer + marks + marks[:1],
            )
            if s + 1 < steps:
                direct, swapped = parts
                swapped = moved(swapped, 0, lambda i: i ^ 1)
                direct = moved(direct, 0, 1)
                relayed = moved(swapped, 0, 2, lambda i: i % 2 == 0)
            else:
                plus = moved(parts[0], 1, 0)
    v = call(
        part(final_kernel, steps - 1), [group], [plus, early, minus], v_shape,
        marks + [pltpu.SemaphoreType.DMA((tiles,))], out_space=HBM,
    )
    return v.reshape(vertex.shape), c.reshape(context.shape)


def solution(mesh):
    return jax.shard_map(
        body,
        mesh=mesh,
        in_specs=(
            P(("outer", "inner"), None),
            P(("outer", "inner"), None),
            P(("outer", "inner")),
            P(("outer", "inner"), None),
            P(("outer", "inner"), None),
            P(("outer", "inner"), None, None),
            P(("outer", "inner"), None, None, None),
        ),
        out_specs=(P(("outer", "inner"), None), P(("outer", "inner"), None)),
        check_vma=False,
    )
```
